32 devices in a mesh: grp: 2 (over x), seq: 16 (over z, y, core).
Axes of the slice: x: 2, y: 2, z: 4, core: 2. Of those that a mesh axis runs over, the one named last changes fastest.
Arguments:
- corpus: bfloat16 [8192, 3584], P(('grp', 'seq')), parts along dimension 0, may hold values from -6 to 6
- window_ends: int32 [64], P(('grp', 'seq')), parts along dimension 0, may hold values from 0 to 255
- norm_gain: float32 [3584], replicated, may hold values from 0.5 to 1.5
- routes: int32 [1024, 2], P(('grp', 'seq')), parts along dimension 0, may hold values from 0 to 15, all different within a row; in each aligned block of 32 rows (0 to 31, 32 to 63, ...) at most 8 rows name the same one
- in_blocks: int32 [16, 7], replicated, may hold values from 0 to 27, all different within a row
- out_blocks: int32 [16, 7], replicated, may hold values from 0 to 27, all different within a row
- enc_weight: bfloat16 [896, 32768], P(None, 'seq'), may hold values from -0.1875 to 0.1875
- enc_bias: float32 [32768], P('seq'), may hold values from -3 to 3
- latent_cutoffs: float32 [32768], P('seq'), may hold values from 0.2 to 1.2
- dec_weight: bfloat16 [32768, 896], P('seq'), may hold values from -0.125 to 0.125
- readout: float32 [32768], P('seq'), may hold values from -1.5 to 1.5
- dec_bias: float32 [3584], replicated, may hold values from -3 to 3
Outputs:
- reconstruction: bfloat16 [8192, 3584], P(('grp', 'seq')), parts along dimension 0
- attribution: bfloat16 [8192, 3584], P(('grp', 'seq')), parts along dimension 0
- feature_score: float32 [8192], P(('grp', 'seq')), parts along dimension 0
The draws below stay inside these ranges and needn't reach their ends.
There are 2 independent parts, one for each index of `grp`. The reference program is written for one: setup_inputs(seed, part) draws one part's arguments, and reference() takes and returns one part's arrays. A program takes and returns all parts, laid end to end along the dimension named above; an argument that names none is the same for every part. Nothing has to cross between parts.
Inputs may be any that keep to these rules, and one draw needn't show every extreme that they name: `routes`: each segment names 2 different feature groups; within the 32 segments of one device no group is named more than 8 times. `in_blocks`: each row names 7 different blocks, and every block is named by some row. `out_blocks`: each row names 7 different blocks, and every block is named by some row.
All inputs are finite; a program needn't handle non-finite values.
Results may differ from the reference program's by a relative error of at most 0.012.
Values may be sent and summed in bfloat16 or wider, within the bound.
No kernel may reach another device: no remote copies, remote signals or barrier semaphores. Data moves between devices by JAX's collectives and lax.ppermute only.
A program may use at most 128 MiB of HBM per device.

```python
import math
import jax
import jax.numpy as jnp
import numpy as np
from jax import lax

D = 3584
BLK = 128
KEEP = 7
FEAT_DEV = 2048
LEN = 128
SEG = 8
TOPK = 2
WIN_DEV = 2
DBLK = 28
CORP_DEV = 256
SEGS = 32
CAP = 8
FEATURES = 32768
WINDOWS = 32
TOKENS = 4096
CORPUS = 4096
SEGMENTS = 512
N_SEQ = 16


def plant(entries, rng, smallest, high):
    index_at = [jax.random.randint(jax.random.fold_in(rng, axis), (), 0, length) for axis, length in enumerate(entries.shape)]
    widest = entries.shape.index(max(entries.shape))
    neighbour = index_at[:widest] + [(index_at[widest] + 1) % entries.shape[widest]] + index_at[widest + 1:]
    return entries.at[tuple(index_at)].set(smallest).at[tuple(neighbour)].set(high)


def block_levels(own_key, extent, pieces, low, top_value):
    def one(position, parts):
        draws = jax.random.uniform(jax.random.fold_in(jax.random.fold_in(own_key, 6), position), (parts,), jnp.float32, low / len(pieces), top_value / len(pieces))
        return jnp.repeat(jnp.exp(draws), extent[position] // parts).reshape((-1,) + (1,) * (len(extent) - position - 1))

    factor_of = one(*pieces[0])
    for cut in pieces[1:]:
        factor_of = factor_of * one(*cut)
    return factor_of


def picks_of(own_key, rows, count, top, lift):
    order = jax.random.permutation(jax.random.fold_in(own_key, 1), count)
    pull = order
    for power in range(3):
        pull = pull * pull // count
    pull = pull * lift // count
    chance = jax.random.randint(jax.random.fold_in(own_key, 2), (rows, count), 0, 4096) + pull
    holders = jax.random.permutation(jax.random.fold_in(own_key, 3), rows)[jnp.arange(count) % rows]
    chance = jnp.where(jnp.arange(rows)[:, None] == holders[None, :], 1 << 14, chance)
    merit = chance * count + jnp.arange(count)
    return lax.top_k(merit.astype(jnp.int32), top)[1].astype(jnp.int32)


def shared_out(key, own, number, rows, count, top, limit, slope):
    sequence = jax.random.permutation(key, count)
    crowded, ordinary = load_shares(count, rows * top, limit, slope, True), load_shares(count, rows * top, limit, slope, False)
    places = jnp.arange(count)

    def named(tallies, rotation):
        used = int((tallies > 0).sum())
        fixed = max(1, used // 4)
        shifted = fixed + (places - fixed + rotation * (used - fixed)) % max(1, count - fixed)
        return jnp.zeros((count,), jnp.int32).at[sequence[jnp.where(places < fixed, places, shifted)]].set(jnp.asarray(tallies, jnp.int32))

    tallies = jnp.where(number % 4 == 0, named(crowded, number // 4), named(ordinary, number - number // 4 - 1))
    mixed = jax.random.permutation(jax.random.fold_in(own, 3), count)
    source_of, taker = mixed[0:count // 2 * 2:2], mixed[1:count // 2 * 2:2]
    margin = jnp.minimum(tallies[source_of] - 1, limit - tallies[taker]) // 2
    margin = jnp.where((source_of == sequence[0]) | (taker == sequence[0]) | (tallies[taker] == 0), 0, jnp.maximum(margin, 0))
    shifted = jax.random.randint(jax.random.fold_in(own, 4), (count // 2,), 0, 1 << 20) % (margin + 1)
    tallies = tallies.at[source_of].add(-shifted).at[taker].add(shifted)
    items = jnp.searchsorted(jnp.cumsum(tallies), jnp.arange(rows * top), side="right").astype(jnp.int32)
    table = items.reshape(top, rows).T
    table = table[jax.random.permutation(jax.random.fold_in(own, 1), rows)]
    rotation = jax.random.randint(jax.random.fold_in(own, 2), (rows, 1), 0, top)
    return jnp.take_along_axis(table, (jnp.arange(top)[None, :] + rotation) % top, axis=1)


def load_shares(number_of, total, limit, lean, full):
    weights = [(1 << 20) // math.isqrt(grade ** lean) + 1 for grade in range(1, number_of + 1)]
    largest = limit if full else min(limit, max(-(-total // number_of), total * weights[0] // sum(weights)))
    least = 1 if total - largest >= number_of - 1 else 0
    counts, spare = [largest] + [least] * (number_of - 1), total - largest - least * (number_of - 1)
    while spare > 0:
        candidates = [i for i in range(1, number_of) if counts[i] < largest] or [i for i in range(1, number_of) if counts[i] < limit]
        whole, left = sum([weights[i] for i in candidates]), spare
        for i in candidates:
            addition = min(limit - counts[i], max(1, left * weights[i] // whole), spare)
            counts[i] = counts[i] + addition
            spare = spare - addition
    return np.array(counts)


def bell_draw(key, extent, width, reach, cuts=(), kind=jnp.bfloat16):
    array = width * jax.random.normal(key, extent, jnp.float32)
    if cuts:
        array = array * block_levels(key, extent, cuts, -0.22, 0.18)
    return jnp.clip(array, -reach, reach).astype(kind)


def setup_inputs(seed: int = 0, part: int = 0) -> dict:
    streams_of = jax.random.split(jax.random.key(seed), 13)
    part_keys = jax.random.split(jax.random.fold_in(streams_of[12], part), 13)
    corpus = bell_draw(part_keys[0], (CORPUS, D), 1.0, 6.0, ((0, 16),))
    window_ends = plant(jax.random.randint(part_keys[1], (WINDOWS,), 0, CORP_DEV), jax.random.fold_in(part_keys[1], 1), 0, CORP_DEV - 1).astype(jnp.int32)
    norm_gain = jnp.clip(1.0 + 0.1 * jax.random.normal(streams_of[2], (D,), jnp.float32), 0.5, 1.5)
    routes_keys = jax.random.split(jax.random.fold_in(part_keys[3], 1), SEGMENTS // SEGS)
    routes_turns = jax.random.permutation(jax.random.fold_in(part_keys[3], 3), SEGMENTS // SEGS)
    routes = jax.vmap(lambda own, number: shared_out(jax.random.fold_in(part_keys[3], 2), own, number, SEGS, N_SEQ, TOPK, CAP, 2))(routes_keys, routes_turns).reshape((SEGMENTS, TOPK))
    in_blocks = picks_of(streams_of[4], N_SEQ, D // BLK, KEEP, 0)
    out_blocks = picks_of(streams_of[5], N_SEQ, D // BLK, KEEP, 0)
    enc_weight = bell_draw(streams_of[6], (KEEP * BLK, FEATURES), (KEEP * BLK) ** -0.5, 0.1875, ((1, 16),))
    enc_bias = bell_draw(streams_of[7], (FEATURES,), 0.5, 3.0, ((0, 16),), jnp.float32)
    latent_cutoffs = jnp.clip(jnp.exp(math.log(1.2) - 1.7917595 * jax.random.uniform(streams_of[8], (FEATURES,), jnp.float32) ** block_levels(streams_of[8], (FEATURES,), ((0, 16),), -0.2, 0.2)), 0.2, 1.2)
    dec_weight = bell_draw(streams_of[9], (FEATURES, KEEP * BLK), FEAT_DEV ** -0.5, 0.125, ((0, 16),))
    readout = bell_draw(streams_of[10], (FEATURES,), 0.25, 1.5, ((0, 16),), jnp.float32)
    dec_bias = bell_draw(streams_of[11], (D,), 0.5, 3.0, (), jnp.float32)
    return dict(corpus=corpus, window_ends=window_ends, norm_gain=norm_gain, routes=routes, in_blocks=in_blocks, out_blocks=out_blocks, enc_weight=enc_weight, enc_bias=enc_bias, latent_cutoffs=latent_cutoffs, dec_weight=dec_weight, readout=readout, dec_bias=dec_bias)


step_sharpness = 0.1
norm_eps = 1e-06

def normalize(rows, norm_gain):
    widened = rows.astype(jnp.float32)
    inverse_rms = lax.rsqrt(lax.optimization_barrier(jnp.mean(widened * widened, axis=-1, keepdims=True)) + norm_eps)
    return (widened * inverse_rms * norm_gain).astype(jnp.bfloat16)

def window_rows(corpus, window_ends):
    padded = jnp.concatenate([jnp.zeros((LEN, D), corpus.dtype), corpus], axis=0)
    owners = jnp.arange(WINDOWS, dtype=jnp.int32) // WIN_DEV * CORP_DEV
    starts = (owners + window_ends + 1).astype(jnp.int32)

    def take_one(start):
        return lax.dynamic_slice_in_dim(padded, start, LEN, 0)
    return jax.vmap(take_one)(starts).reshape(WINDOWS * LEN, D)

def group_terms(segment, group_id, in_blocks, out_blocks, enc_weight, enc_bias, latent_cutoffs, dec_weight, readout):
    input_ids = in_blocks[group_id]
    output_ids = out_blocks[group_id]
    first = (group_id * FEAT_DEV).astype(jnp.int32)
    blocks = segment.reshape(SEG, DBLK, BLK)
    chosen = jnp.take(blocks, input_ids, axis=1).reshape(SEG, KEEP * BLK)
    enc_slice = lax.dynamic_slice_in_dim(enc_weight, first, FEAT_DEV, 1)
    dec_slice = lax.dynamic_slice_in_dim(dec_weight, first, FEAT_DEV, 0)
    bias_slice = lax.dynamic_slice_in_dim(enc_bias, first, FEAT_DEV, 0)
    cutoff_contribution = lax.dynamic_slice_in_dim(latent_cutoffs, first, FEAT_DEV, 0)
    output_contribution = lax.dynamic_slice_in_dim(readout, first, FEAT_DEV, 0)
    latent_input_level = jnp.dot(chosen, enc_slice, preferred_element_type=jnp.float32) + bias_slice
    exceeds_cutoff_indicator = jax.nn.sigmoid((latent_input_level - cutoff_contribution) / step_sharpness)
    nonzero_latent_count = latent_input_level * exceeds_cutoff_indicator
    active_half = nonzero_latent_count.astype(jnp.bfloat16)
    decoded = jnp.dot(active_half, dec_slice, preferred_element_type=jnp.float32).astype(jnp.bfloat16)
    score_term = lax.optimization_barrier(jnp.sum(nonzero_latent_count * output_contribution, axis=-1)).astype(jnp.bfloat16)
    midpoint_gradient = (output_contribution * (exceeds_cutoff_indicator + latent_input_level * exceeds_cutoff_indicator * (1.0 - exceeds_cutoff_indicator) / step_sharpness)).astype(jnp.bfloat16)
    pulled = jnp.dot(midpoint_gradient, enc_slice.T, preferred_element_type=jnp.float32).astype(jnp.bfloat16)
    placed_out = jnp.zeros((SEG, DBLK, BLK), jnp.float32).at[:, output_ids].set(decoded.astype(jnp.float32).reshape(SEG, KEEP, BLK))
    placed_in = jnp.zeros((SEG, DBLK, BLK), jnp.float32).at[:, input_ids].set(pulled.astype(jnp.float32).reshape(SEG, KEEP, BLK))
    return (placed_out.reshape(SEG, D), placed_in.reshape(SEG, D), score_term.astype(jnp.float32))

def reference(corpus, window_ends, norm_gain, routes, in_blocks, out_blocks, enc_weight, enc_bias, latent_cutoffs, dec_weight, readout, dec_bias):
    normal = normalize(window_rows(corpus, window_ends), norm_gain)
    segments = normal.reshape(SEGMENTS, SEG, D)

    def per_segment(packed):
        segment, route_row = packed
        recon_sum = jnp.zeros((SEG, D), jnp.float32)
        grad_sum = jnp.zeros((SEG, D), jnp.float32)
        score_sum = jnp.zeros((SEG,), jnp.float32)
        for route_slot in range(TOPK):
            decoded, pulled, score_term = group_terms(segment, route_row[route_slot], in_blocks, out_blocks, enc_weight, enc_bias, latent_cutoffs, dec_weight, readout)
            recon_sum = recon_sum + decoded
            grad_sum = grad_sum + pulled
            score_sum = score_sum + score_term
        return (recon_sum, grad_sum, score_sum)
    recon_sum, grad_sum, score_sum = lax.map(per_segment, (segments, routes))
    reconstruction = (recon_sum.reshape(TOKENS, D) + dec_bias).astype(jnp.bfloat16)
    attribution = (normal.astype(jnp.float32) * grad_sum.reshape(TOKENS, D)).astype(jnp.bfloat16)
    return (reconstruction, attribution, score_sum.reshape(TOKENS))
```

```python
import functools

import jax
import jax.numpy as jnp
from jax import lax
from jax.experimental import pallas as pl
from jax.experimental.pallas import tpu as pltpu
from jax.sharding import PartitionSpec as P

BLK = 128
KEEP = 7
LEN = 128
SEG = 8
step_sharpness = 0.1
norm_eps = 1e-06


SMEM = pl.BlockSpec(memory_space=pltpu.SMEM)
VMEM = pl.BlockSpec(memory_space=pltpu.VMEM)
ANY = pl.BlockSpec(memory_space=pl.ANY)


def clear_counts(counts, groups):
    def zero(i, carry):
        counts[i] = 0
        return carry

    lax.fori_loop(0, groups, zero, 0)


def pack_kernel(groups, cap, fanout, windows, *refs):
    me_ref, ends_ref, routes_ref, in_ref, gain_ref, corpus_ref, below_ref = refs[:7]
    normal_ref = refs[7]
    outs = refs[8 : 8 + groups]
    ext, stage, counts, sems = refs[8 + groups :]
    own_rows, width = corpus_ref.shape
    gain = gain_ref[...]

    def normalize_rows(source, base):
        def body(i, carry):
            at = pl.multiple_of(i * 16, 16)
            x = source[pl.ds(at, 16), :].astype(jnp.float32)
            mean = jnp.sum(x * x, axis=1, keepdims=True) * (1.0 / width)
            y = (x * lax.rsqrt(mean + norm_eps) * gain).astype(jnp.bfloat16)
            ext[pl.ds(pl.multiple_of(base + i * 16, 16), 16), :] = y.astype(jnp.float32)
            return carry

        lax.fori_loop(0, source.shape[0] // 16, body, 0)

    normalize_rows(corpus_ref, LEN)
    normalize_rows(below_ref, 0)
    segs_per_window = LEN // SEG
    last = ext.shape[0] - SEG
    sublane = lax.broadcasted_iota(jnp.int32, (SEG, width), 0)
    for w in range(windows):
        first = ends_ref[w] + 1
        offset = lax.rem(first, SEG)
        base = first - offset
        turn = lax.rem(SEG - offset, SEG)

        def take(j, carry):
            low = pl.multiple_of(base + j * SEG, SEG)
            high = pl.multiple_of(jnp.minimum(low + SEG, last), SEG)
            rows = jnp.where(
                sublane < SEG - offset,
                pltpu.roll(ext[pl.ds(low, SEG), :], turn, 0),
                pltpu.roll(ext[pl.ds(high, SEG), :], turn, 0),
            )
            normal_ref[w * segs_per_window + j] = rows.astype(jnp.bfloat16)
            return carry

        lax.fori_loop(0, segs_per_window, take, 0)
    clear_counts(counts, groups)
    me = me_ref[0]

    def place(t, carry):
        for k in range(fanout):
            group = routes_ref[t * fanout + k]
            slot = counts[group]
            counts[group] = slot + 1
            partner = group ^ me
            for q in range(KEEP):
                at = pl.multiple_of(in_ref[group * KEEP + q] * BLK, BLK)
                stage[partner, q, slot] = normal_ref[t, :, pl.ds(at, BLK)]
        return carry

    lax.fori_loop(0, windows * segs_per_window, place, 0)
    copies = [
        pltpu.make_async_copy(stage.at[s], outs[s], sems.at[s]) for s in range(groups)
    ]
    for copy in copies:
        copy.start()
    for copy in copies:
        copy.wait()


def features_kernel(count, cap, *refs):
    xs = refs[:count]
    enc_ref, dec_ref, bias_ref, cut_ref, read_ref = refs[count : count + 5]
    outs = refs[count + 5 : 2 * count + 5]
    x_all, dec_acc, pull_acc, score_acc = refs[2 * count + 5 :]
    step = pl.program_id(0)
    rows = cap * SEG

    @pl.when(step == 0)
    def _():
        for i in range(count):
            for q in range(KEEP):
                x_all[i * rows : (i + 1) * rows, q * BLK : (q + 1) * BLK] = xs[i][q]
        dec_acc[...] = jnp.zeros_like(dec_acc)
        pull_acc[...] = jnp.zeros_like(pull_acc)
        score_acc[...] = jnp.zeros_like(score_acc)

    pre = (
        jnp.dot(x_all[...], enc_ref[...], preferred_element_type=jnp.float32) + bias_ref[...]
    )
    readout = read_ref[...]
    firing = jax.nn.sigmoid((pre - cut_ref[...]) * (1.0 / step_sharpness))
    active = pre * firing
    slope = (
        readout * (firing + active * (1.0 - firing) * (1.0 / step_sharpness))
    ).astype(jnp.bfloat16)
    dec_acc[...] += jnp.dot(
        active.astype(jnp.bfloat16), dec_ref[...], preferred_element_type=jnp.float32
    )
    pull_acc[...] += lax.dot_general(
        slope, enc_ref[...], (((1,), (1,)), ((), ())), preferred_element_type=jnp.float32
    )
    weighted = readout * active
    part = weighted[:, :BLK]
    for j in range(1, weighted.shape[1] // BLK):
        part = part + weighted[:, j * BLK : (j + 1) * BLK]
    score_acc[...] += part

    @pl.when(step == pl.num_programs(0) - 1)
    def _():
        lanes = lax.broadcasted_iota(jnp.int32, (SEG, BLK), 1)
        totals = jnp.sum(score_acc[...], axis=1, keepdims=True)
        for i in range(count):
            for q in range(KEEP):
                for acc, base in ((dec_acc, 0), (pull_acc, KEEP)):
                    tile = acc[i * rows : (i + 1) * rows, q * BLK : (q + 1) * BLK]
                    outs[i][(base + q) * cap : (base + q + 1) * cap] = tile.astype(
                        jnp.bfloat16
                    ).reshape(cap, SEG, BLK)
            marks = jnp.zeros((SEG, BLK), jnp.float32)
            for c in range(cap):
                at = i * rows + c * SEG
                marks = jnp.where(lanes == c, totals[at : at + SEG], marks)
            outs[i][2 * KEEP * cap] = marks.astype(jnp.bfloat16)


def combine_kernel(groups, cap, fanout, segments, *refs):
    me_ref, routes_ref, in_ref, out_ref, bias_ref, normal_ref = refs[:6]
    backs = refs[6 : 6 + groups]
    recon_ref, attr_ref, score_ref = refs[6 + groups : 9 + groups]
    stage, recon_acc, grad_acc, counts, sems = refs[9 + groups :]
    copies = [
        pltpu.make_async_copy(backs[s], stage.at[s], sems.at[s]) for s in range(groups)
    ]
    for copy in copies:
        copy.start()
    clear_counts(counts, groups)
    me = me_ref[0]
    for copy in copies:
        copy.wait()
    lanes = lax.broadcasted_iota(jnp.int32, (SEG, BLK), 1)
    bias = jnp.broadcast_to(bias_ref[...], recon_acc.shape)

    def one(t, scores):
        recon_acc[...] = bias
        grad_acc[...] = jnp.zeros_like(grad_acc)
        total = jnp.zeros((SEG, 1), jnp.float32)
        for k in range(fanout):
            group = routes_ref[t * fanout + k]
            slot = counts[group]
            counts[group] = slot + 1
            partner = group ^ me
            for q in range(KEEP):
                at = pl.multiple_of(out_ref[group * KEEP + q] * BLK, BLK)
                recon_acc[:, pl.ds(at, BLK)] += stage[partner, q * cap + slot].astype(
                    jnp.float32
                )
                at = pl.multiple_of(in_ref[group * KEEP + q] * BLK, BLK)
                grad_acc[:, pl.ds(at, BLK)] += stage[
                    partner, (KEEP + q) * cap + slot
                ].astype(jnp.float32)
            marks = stage[partner, 2 * KEEP * cap].astype(jnp.float32)
            total = total + jnp.sum(
                jnp.where(lanes == slot, marks, 0.0), axis=1, keepdims=True
            )
        recon_ref[t] = recon_acc[...].astype(jnp.bfloat16)
        attr_ref[t] = (normal_ref[t].astype(jnp.float32) * grad_acc[...]).astype(
            jnp.bfloat16
        )
        return jnp.where(lanes == t, total, scores)

    score_ref[...] = lax.fori_loop(0, segments, one, jnp.zeros((SEG, BLK), jnp.float32))


def shards(
    corpus,
    window_ends,
    norm_gain,
    routes,
    in_blocks,
    out_blocks,
    enc_weight,
    enc_bias,
    latent_cutoffs,
    dec_weight,
    readout,
    dec_bias,
):
    groups = lax.axis_size("seq")
    width = corpus.shape[1]
    windows = window_ends.shape[0]
    segments, fanout = routes.shape
    features = enc_weight.shape[1]
    cap = max(2, 2 * segments * fanout // groups)
    me = lax.axis_index("seq").astype(jnp.int32).reshape(1)
    below = lax.ppermute(corpus[-LEN:], "seq", [(i, i + 1) for i in range(groups - 1)])
    flat_routes = routes.reshape(-1)
    flat_in = in_blocks.reshape(-1)
    flat_out = out_blocks.reshape(-1)

    packed = pl.pallas_call(
        functools.partial(pack_kernel, groups, cap, fanout, windows),
        out_shape=(jax.ShapeDtypeStruct((segments, SEG, width), jnp.bfloat16),)
        + (jax.ShapeDtypeStruct((KEEP, cap, SEG, BLK), jnp.bfloat16),) * groups,
        in_specs=[SMEM] * 4 + [VMEM] * 3,
        out_specs=(VMEM,) + (ANY,) * groups,
        scratch_shapes=[
            pltpu.VMEM((LEN + corpus.shape[0], width), jnp.float32),
            pltpu.VMEM((groups, KEEP, cap, SEG, BLK), jnp.bfloat16),
            pltpu.SMEM((groups,), jnp.int32),
            pltpu.SemaphoreType.DMA((groups,)),
        ],
        cost_estimate=pl.CostEstimate(flops=10_000_000, bytes_accessed=8_000_000, transcendentals=0),
        name="pack",
    )(me, window_ends, flat_routes, flat_in, norm_gain.reshape(1, -1), corpus, below)
    normal, outgoing = packed[0], packed[1:]

    def exchange(block, pattern):
        if pattern == 0:
            return block
        return lax.ppermute(block, "seq", [(i, i ^ pattern) for i in range(groups)])

    quarter = groups // 4
    order = [2, 3, 1, 0]
    arrived = {}
    for part in order:
        for s in range(part * quarter, (part + 1) * quarter):
            arrived[s] = exchange(outgoing[s], s)

    rows = cap * SEG
    tile = 512
    features_call = pl.pallas_call(
        functools.partial(features_kernel, quarter, cap),
        grid=(features // tile,),
        out_shape=(
            jax.ShapeDtypeStruct((2 * KEEP * cap + 1, SEG, BLK), jnp.bfloat16),
        )
        * quarter,
        in_specs=[pl.BlockSpec((KEEP, rows, BLK), lambda f: (0, 0, 0))] * quarter
        + [
            pl.BlockSpec((KEEP * BLK, tile), lambda f: (0, f)),
            pl.BlockSpec((tile, KEEP * BLK), lambda f: (f, 0)),
            pl.BlockSpec((1, tile), lambda f: (0, f)),
            pl.BlockSpec((1, tile), lambda f: (0, f)),
            pl.BlockSpec((1, tile), lambda f: (0, f)),
        ],
        out_specs=(
            pl.BlockSpec((2 * KEEP * cap + 1, SEG, BLK), lambda f: (0, 0, 0)),
        )
        * quarter,
        scratch_shapes=[
            pltpu.VMEM((quarter * rows, KEEP * BLK), jnp.bfloat16),
            pltpu.VMEM((quarter * rows, KEEP * BLK), jnp.float32),
            pltpu.VMEM((quarter * rows, KEEP * BLK), jnp.float32),
            pltpu.VMEM((quarter * rows, BLK), jnp.float32),
        ],
        cost_estimate=pl.CostEstimate(
            flops=6 * quarter * rows * KEEP * BLK * features,
            bytes_accessed=4 * KEEP * BLK * features,
            transcendentals=quarter * rows * features,
        ),
        name="features",
    )
    returned = {}
    for part in order:
        members = list(range(part * quarter, (part + 1) * quarter))
        results = features_call(
            *[arrived[s].reshape(KEEP, rows, BLK) for s in members],
            enc_weight,
            dec_weight,
            enc_bias.reshape(1, -1),
            latent_cutoffs.reshape(1, -1),
            readout.reshape(1, -1),
        )
        for s, result in zip(members, results):
            returned[s] = exchange(result, s)

    recon, attr, score = pl.pallas_call(
        functools.partial(combine_kernel, groups, cap, fanout, segments),
        out_shape=(
            jax.ShapeDtypeStruct((segments, SEG, width), jnp.bfloat16),
            jax.ShapeDtypeStruct((segments, SEG, width), jnp.bfloat16),
            jax.ShapeDtypeStruct((SEG, BLK), jnp.float32),
        ),
        in_specs=[SMEM] * 4 + [VMEM] * 2 + [ANY] * groups,
        out_specs=(VMEM,) * 3,
        scratch_shapes=[
            pltpu.VMEM((groups, 2 * KEEP * cap + 1, SEG, BLK), jnp.bfloat16),
            pltpu.VMEM((SEG, width), jnp.float32),
            pltpu.VMEM((SEG, width), jnp.float32),
            pltpu.SMEM((groups,), jnp.int32),
            pltpu.SemaphoreType.DMA((groups,)),
        ],
        cost_estimate=pl.CostEstimate(flops=10_000_000, bytes_accessed=8_000_000, transcendentals=0),
        name="combine",
    )(
        me,
        flat_routes,
        flat_in,
        flat_out,
        dec_bias.reshape(1, -1),
        normal,
        *[returned[s] for s in range(groups)],
    )
    feature_score = score[:, :segments].T.reshape(-1)
    return (recon.reshape(-1, width), attr.reshape(-1, width), feature_score)


def solution(mesh):
    in_specs = (
        P(("grp", "seq"), None),
        P(("grp", "seq")),
        P(),
        P(("grp", "seq"), None),
        P(),
        P(),
        P(None, "seq"),
        P("seq"),
        P("seq"),
        P("seq", None),
        P("seq"),
        P(),
    )
    out_specs = (P(("grp", "seq"), None), P(("grp", "seq"), None), P(("grp", "seq")))
    return jax.shard_map(shards, mesh=mesh, in_specs=in_specs, out_specs=out_specs, check_vma=False)
```

```python
import functools

import jax
import jax.numpy as jnp
from jax import lax
from jax.experimental import pallas as pl
from jax.experimental.pallas import tpu as pltpu
from jax.sharding import PartitionSpec as P

BLK = 128
KEEP = 7
LEN = 128
SEG = 8
step_sharpness = 0.1
norm_eps = 1e-06


SMEM = pl.BlockSpec(memory_space=pltpu.SMEM)
VMEM = pl.BlockSpec(memory_space=pltpu.VMEM)
ANY = pl.BlockSpec(memory_space=pl.ANY)


def clear_counts(counts, groups):
    def zero(i, carry):
        counts[i] = 0
        return carry

    lax.fori_loop(0, groups, zero, 0)


def normalize_rows(x, gain, width):
    x = x.astype(jnp.float32)
    mean = jnp.sum(x * x, axis=1, keepdims=True) * (1.0 / width)
    return (x * lax.rsqrt(mean + norm_eps) * gain).astype(jnp.bfloat16).astype(jnp.float32)


def own_kernel(gain_ref, corpus_ref, own_ref):
    rows, width = corpus_ref.shape
    gain = gain_ref[...]

    def body(i, carry):
        at = pl.ds(pl.multiple_of(i * 16, 16), 16)
        own_ref[at, :] = normalize_rows(corpus_ref[at, :], gain, width)
        return carry

    lax.fori_loop(0, rows // 16, body, 0)


def pack_kernel(groups, cap, fanout, windows, *refs):
    me_ref, ends_ref, routes_ref, in_ref, gain_ref, own_ref, below_ref = refs[:7]
    normal_ref = refs[7]
    outs = refs[8 : 8 + groups]
    ext, stage, counts, sems = refs[8 + groups :]
    width = own_ref.shape[1]
    gain = gain_ref[...]

    def body(i, carry):
        at = pl.ds(pl.multiple_of(i * 16, 16), 16)
        ext[at, :] = normalize_rows(below_ref[at, :], gain, width)
        return carry

    lowest = ends_ref[0] + 1
    for w in range(1, windows):
        lowest = jnp.minimum(lowest, ends_ref[w] + 1)
    lax.fori_loop(jnp.minimum(lowest, LEN) // 16, LEN // 16, body, 0)
    ext[LEN:, :] = own_ref[:SEG, :]
    clear_counts(counts, groups)
    me = me_ref[0]
    segs_per_window = LEN // SEG
    last = own_ref.shape[0] - SEG
    sublane = lax.broadcasted_iota(jnp.int32, (SEG, width), 0)
    for w in range(windows):
        first = ends_ref[w] + 1
        offset = lax.rem(first, SEG)
        base = first - offset
        turn = lax.rem(SEG - offset, SEG)

        def place(j, low_rows, high_rows):
            t = w * segs_per_window + j
            rows = jnp.where(
                sublane < SEG - offset,
                pltpu.roll(low_rows, turn, 0),
                pltpu.roll(high_rows, turn, 0),
            )
            normal_ref[t] = rows.astype(jnp.bfloat16)
            for k in range(fanout):
                group = routes_ref[t * fanout + k]
                slot = counts[group]
                counts[group] = slot + 1
                partner = group ^ me
                for q in range(KEEP):
                    at = pl.multiple_of(in_ref[group * KEEP + q] * BLK, BLK)
                    stage[partner, q, slot] = normal_ref[t, :, pl.ds(at, BLK)]

        def from_below(j, carry):
            low = pl.multiple_of(base + j * SEG, SEG)
            place(j, ext[pl.ds(low, SEG), :], ext[pl.ds(low + SEG, SEG), :])
            return carry

        def from_own(j, carry):
            low = pl.multiple_of(base + j * SEG - LEN, SEG)
            high = pl.multiple_of(jnp.minimum(low + SEG, last), SEG)
            place(j, own_ref[pl.ds(low, SEG), :], own_ref[pl.ds(high, SEG), :])
            return carry

        split = jnp.clip((LEN - base) // SEG, 0, segs_per_window)
        lax.fori_loop(0, split, from_below, 0)
        lax.fori_loop(split, segs_per_window, from_own, 0)
    copies = [
        pltpu.make_async_copy(stage.at[s], outs[s], sems.at[s]) for s in range(groups)
    ]
    for copy in copies:
        copy.start()
    for copy in copies:
        copy.wait()


def features_kernel(count, cap, *refs):
    xs = refs[:count]
    enc_ref, dec_ref, bias_ref, cut_ref, read_ref = refs[count : count + 5]
    outs = refs[count + 6 : 2 * count + 6]
    x_all, dec_acc, pull_acc, score_acc = refs[2 * count + 6 :]
    step = pl.program_id(0)
    rows = cap * SEG

    @pl.when(step == 0)
    def _():
        for i in range(count):
            for q in range(KEEP):
                x_all[i * rows : (i + 1) * rows, q * BLK : (q + 1) * BLK] = xs[i][q]
        dec_acc[...] = jnp.zeros_like(dec_acc)
        pull_acc[...] = jnp.zeros_like(pull_acc)
        score_acc[...] = jnp.zeros_like(score_acc)

    pre = (
        jnp.dot(x_all[...], enc_ref[...], preferred_element_type=jnp.float32) + bias_ref[...]
    )
    readout = read_ref[...]
    firing = jax.nn.sigmoid((pre - cut_ref[...]) * (1.0 / step_sharpness))
    active = pre * firing
    slope = (
        readout * (firing + active * (1.0 - firing) * (1.0 / step_sharpness))
    ).astype(jnp.bfloat16)
    dec_acc[...] += jnp.dot(
        active.astype(jnp.bfloat16), dec_ref[...], preferred_element_type=jnp.float32
    )
    pull_acc[...] += lax.dot_general(
        slope, enc_ref[...], (((1,), (1,)), ((), ())), preferred_element_type=jnp.float32
    )
    weighted = readout * active
    part = weighted[:, :BLK]
    for j in range(1, weighted.shape[1] // BLK):
        part = part + weighted[:, j * BLK : (j + 1) * BLK]
    score_acc[...] += part

    @pl.when(step == pl.num_programs(0) - 1)
    def _():
        lanes = lax.broadcasted_iota(jnp.int32, (SEG, BLK), 1)
        totals = jnp.sum(score_acc[...], axis=1, keepdims=True)
        for i in range(count):
            for q in range(KEEP):
                for acc, base in ((dec_acc, 0), (pull_acc, KEEP)):
                    tile = acc[i * rows : (i + 1) * rows, q * BLK : (q + 1) * BLK]
                    outs[i][(base + q) * cap : (base + q + 1) * cap] = tile.astype(
                        jnp.bfloat16
                    ).reshape(cap, SEG, BLK)
            marks = jnp.zeros((SEG, BLK), jnp.float32)
            for c in range(cap):
                at = i * rows + c * SEG
                marks = jnp.where(lanes == c, totals[at : at + SEG], marks)
            outs[i][2 * KEEP * cap] = marks.astype(jnp.bfloat16)


def combine_kernel(groups, cap, fanout, segments, final, *refs):
    members = groups // 4 if final else groups - groups // 4
    me_ref, routes_ref, in_ref, out_ref = refs[:4]
    backs = refs[4 : 4 + members]
    if final:
        recon_in, grad_in, score_in, normal_ref = refs[4 + members : 8 + members]
        recon_ref, attr_ref, score_ref = refs[8 + members : 11 + members]
        stage, recon_acc, grad_acc, marks_acc, counts, sems = refs[11 + members :]
    else:
        bias_ref = refs[4 + members]
        recon_acc, grad_acc, score_ref = refs[5 + members : 8 + members]
        stage, counts, sems = refs[8 + members :]
    copies = [
        pltpu.make_async_copy(backs[s], stage.at[s], sems.at[s]) for s in range(members)
    ]
    for copy in copies:
        copy.start()
    clear_counts(counts, groups)
    me = me_ref[0]
    lowest = groups - members if final else 0
    for copy in copies:
        copy.wait()
    lane = lax.broadcasted_iota(jnp.int32, (SEG, BLK), 1)
    sublane = lax.broadcasted_iota(jnp.int32, (SEG, BLK), 0)
    per_row = BLK // SEG
    if not final:
        bias = jnp.broadcast_to(bias_ref[...], recon_acc.shape[1:])

    def one(t, carry):
        if final:
            acc_r, acc_g = recon_acc, grad_acc
            acc_r[0] = recon_in[t]
            acc_g[0] = grad_in[t]
            marks_acc[t] = score_in[t]
            at_t = 0
        else:
            acc_r, acc_g = recon_acc, grad_acc
            acc_r[t] = bias
            acc_g[t] = jnp.zeros_like(bias)
            at_t = t
            score_ref[t] = jnp.zeros((SEG, BLK), jnp.float32)
        for k in range(fanout):
            group = routes_ref[t * fanout + k]
            slot = counts[group]
            counts[group] = slot + 1
            partner = (group ^ me) - lowest
            here = jnp.logical_and(partner >= 0, partner < members)

            @pl.when(here)
            def _():
                for q in range(KEEP):
                    at = pl.ds(pl.multiple_of(out_ref[group * KEEP + q] * BLK, BLK), BLK)
                    acc_r[at_t, :, at] += stage[partner, q * cap + slot].astype(jnp.float32)
                    at = pl.ds(pl.multiple_of(in_ref[group * KEEP + q] * BLK, BLK), BLK)
                    acc_g[at_t, :, at] += stage[partner, (KEEP + q) * cap + slot].astype(
                        jnp.float32
                    )
                marks = stage[partner, 2 * KEEP * cap].astype(jnp.float32)
                held = marks_acc if final else score_ref
                held[t] += jnp.where(lane == slot, marks, 0.0)

        if final:
            recon_ref[t] = acc_r[0].astype(jnp.bfloat16)
            attr_ref[t] = (normal_ref[t].astype(jnp.float32) * acc_g[0]).astype(jnp.bfloat16)
        return carry

    lax.fori_loop(0, segments, one, 0)
    if final:
        for row in range(segments // per_row):
            line = jnp.zeros((SEG, BLK), jnp.float32)
            for i in range(per_row):
                total = jnp.sum(marks_acc[row * per_row + i], axis=1, keepdims=True)
                line = jnp.where(lane == i * SEG + sublane, total, line)
            score_ref[row : row + 1, :] = jnp.sum(line, axis=0, keepdims=True)


def shards(
    corpus,
    window_ends,
    norm_gain,
    routes,
    in_blocks,
    out_blocks,
    enc_weight,
    enc_bias,
    latent_cutoffs,
    dec_weight,
    readout,
    dec_bias,
):
    groups = lax.axis_size("seq")
    width = corpus.shape[1]
    windows = window_ends.shape[0]
    segments, fanout = routes.shape
    features = enc_weight.shape[1]
    cap = max(2, 2 * segments * fanout // groups)
    me = lax.axis_index("seq").astype(jnp.int32).reshape(1)
    below = lax.ppermute(corpus[-LEN:], "seq", [(i, i + 1) for i in range(groups - 1)])
    flat_routes = routes.reshape(-1)
    flat_in = in_blocks.reshape(-1)
    flat_out = out_blocks.reshape(-1)

    own = pl.pallas_call(
        own_kernel,
        out_shape=jax.ShapeDtypeStruct(corpus.shape, jnp.float32),
        in_specs=[VMEM] * 2,
        out_specs=VMEM,
        cost_estimate=pl.CostEstimate(
            flops=6 * corpus.size, bytes_accessed=6 * corpus.size, transcendentals=0
        ),
        compiler_params=pltpu.CompilerParams(vmem_limit_bytes=12 << 20),
        name="own",
    )(norm_gain.reshape(1, -1), corpus)
    packed = pl.pallas_call(
        functools.partial(pack_kernel, groups, cap, fanout, windows),
        out_shape=(jax.ShapeDtypeStruct((segments, SEG, width), jnp.bfloat16),)
        + (jax.ShapeDtypeStruct((KEEP, cap, SEG, BLK), jnp.bfloat16),) * groups,
        in_specs=[SMEM] * 4 + [VMEM] * 3,
        out_specs=(VMEM,) + (ANY,) * groups,
        scratch_shapes=[
            pltpu.VMEM((LEN + SEG, width), jnp.float32),
            pltpu.VMEM((groups, KEEP, cap, SEG, BLK), jnp.bfloat16),
            pltpu.SMEM((groups,), jnp.int32),
            pltpu.SemaphoreType.DMA((groups,)),
        ],
        cost_estimate=pl.CostEstimate(flops=10_000_000, bytes_accessed=8_000_000, transcendentals=0),
        compiler_params=pltpu.CompilerParams(vmem_limit_bytes=16 << 20),
        name="pack",
    )(me, window_ends, flat_routes, flat_in, norm_gain.reshape(1, -1), own, below)
    normal, outgoing = packed[0], packed[1:]

    def exchange(block, pattern):
        if pattern == 0:
            return block
        return lax.ppermute(block, "seq", [(i, i ^ pattern) for i in range(groups)])

    quarter = groups // 4
    order = [2, 3, 1, 0]
    arrived = {}
    for part in order:
        for s in range(part * quarter, (part + 1) * quarter):
            arrived[s] = exchange(outgoing[s], s)

    rows = cap * SEG
    tile = 512
    features_call = pl.pallas_call(
        functools.partial(features_kernel, quarter, cap),
        grid=(features // tile,),
        out_shape=(
            jax.ShapeDtypeStruct((2 * KEEP * cap + 1, SEG, BLK), jnp.bfloat16),
        )
        * quarter,
        in_specs=[pl.BlockSpec((KEEP, rows, BLK), lambda f: (0, 0, 0))] * quarter
        + [
            pl.BlockSpec((KEEP * BLK, tile), lambda f: (0, f)),
            pl.BlockSpec((tile, KEEP * BLK), lambda f: (f, 0)),
            pl.BlockSpec((1, tile), lambda f: (0, f)),
            pl.BlockSpec((1, tile), lambda f: (0, f)),
            pl.BlockSpec((1, tile), lambda f: (0, f)),
            ANY,
        ],
        out_specs=(
            pl.BlockSpec((2 * KEEP * cap + 1, SEG, BLK), lambda f: (0, 0, 0)),
        )
        * quarter,
        scratch_shapes=[
            pltpu.VMEM((quarter * rows, KEEP * BLK), jnp.bfloat16),
            pltpu.VMEM((quarter * rows, KEEP * BLK), jnp.float32),
            pltpu.VMEM((quarter * rows, KEEP * BLK), jnp.float32),
            pltpu.VMEM((quarter * rows, BLK), jnp.float32),
        ],
        cost_estimate=pl.CostEstimate(
            flops=6 * quarter * rows * KEEP * BLK * features,
            bytes_accessed=4 * KEEP * BLK * features,
            transcendentals=quarter * rows * features,
        ),
        compiler_params=pltpu.CompilerParams(vmem_limit_bytes=20 << 20),
        name="features",
    )
    returned = {}
    turn = me
    for part in [2, 0, 1, 3]:
        members = list(range(part * quarter, (part + 1) * quarter))
        results = features_call(
            *[arrived[s].reshape(KEEP, rows, BLK) for s in members],
            enc_weight,
            dec_weight,
            enc_bias.reshape(1, -1),
            latent_cutoffs.reshape(1, -1),
            readout.reshape(1, -1),
            turn,
        )
        turn = results[0]
        for s, result in zip(members, results):
            returned[s] = exchange(result, s)

    def combine(final, members, out_shape, extra_specs, extra_scratch, *rest):
        return pl.pallas_call(
            functools.partial(combine_kernel, groups, cap, fanout, segments, final),
            out_shape=out_shape,
            in_specs=[SMEM] * 4 + [ANY] * len(members) + extra_specs,
            out_specs=(VMEM,) * 3,
            scratch_shapes=[
                pltpu.VMEM((len(members), 2 * KEEP * cap + 1, SEG, BLK), jnp.bfloat16),
                *extra_scratch,
                pltpu.SMEM((groups,), jnp.int32),
                pltpu.SemaphoreType.DMA((len(members),)),
            ],
            cost_estimate=pl.CostEstimate(
                flops=10_000_000, bytes_accessed=10_000_000, transcendentals=0
            ),
            compiler_params=pltpu.CompilerParams(vmem_limit_bytes=24 << 20),
            name="combine",
        )(
            me,
            flat_routes,
            flat_in,
            flat_out,
            *[returned[s] for s in members],
            *rest,
        )

    wide = jax.ShapeDtypeStruct((segments, SEG, width), jnp.float32)
    thin = jax.ShapeDtypeStruct((segments, SEG, width), jnp.bfloat16)
    recon_part, grad_part, score_part = combine(
        False,
        range(groups - quarter),
        (wide, wide, jax.ShapeDtypeStruct((segments, SEG, BLK), jnp.float32)),
        [VMEM],
        [],
        dec_bias.reshape(1, -1),
    )
    recon, attr, score = combine(
        True,
        range(groups - quarter, groups),
        (thin, thin, jax.ShapeDtypeStruct((segments * SEG // BLK, BLK), jnp.float32)),
        [VMEM] * 4,
        [pltpu.VMEM((1, SEG, width), jnp.float32)] * 2
        + [pltpu.VMEM((segments, SEG, BLK), jnp.float32)],
        recon_part,
        grad_part,
        score_part,
        normal,
    )
    feature_score = score.reshape(-1)
    return (recon.reshape(-1, width), attr.reshape(-1, width), feature_score)


def solution(mesh):
    in_specs = (
        P(("grp", "seq"), None),
        P(("grp", "seq")),
        P(),
        P(("grp", "seq"), None),
        P(),
        P(),
        P(None, "seq"),
        P("seq"),
        P("seq"),
        P("seq", None),
        P("seq"),
        P(),
    )
    out_specs = (P(("grp", "seq"), None), P(("grp", "seq"), None), P(("grp", "seq")))
    return jax.shard_map(shards, mesh=mesh, in_specs=in_specs, out_specs=out_specs, check_vma=False)
```

```python
import functools

import jax
import jax.numpy as jnp
from jax import lax
from jax.experimental import pallas as pl
from jax.experimental.pallas import tpu as pltpu
from jax.sharding import PartitionSpec as P


BLK = 128
KEEP = 7
LEN = 128
SEG = 8
step_sharpness = 0.1
norm_eps = 1e-06
PIECES = 4


SMEM = pl.BlockSpec(memory_space=pltpu.SMEM)
VMEM = pl.BlockSpec(memory_space=pltpu.VMEM)
ANY = pl.BlockSpec(memory_space=pl.ANY)


def send_order(groups):
    quarter = groups // 4
    return [s for part in (2, 1, 3, 0) for s in range(part * quarter, (part + 1) * quarter)]


def clear_counts(counts, groups):
    def zero(i, carry):
        counts[i] = 0
        return carry

    lax.fori_loop(0, groups, zero, 0)


def normalize_rows(x, gain, width):
    x = x.astype(jnp.float32)
    mean = jnp.sum(x * x, axis=1, keepdims=True) * (1.0 / width)
    return (x * lax.rsqrt(mean + norm_eps) * gain).astype(jnp.bfloat16).astype(jnp.float32)


def own_kernel(gain_ref, corpus_ref, own_ref):
    rows, width = corpus_ref.shape
    gain = gain_ref[...]

    def body(i, carry):
        at = pl.ds(pl.multiple_of(i * 16, 16), 16)
        own_ref[at, :] = normalize_rows(corpus_ref[at, :], gain, width)
        return carry

    lax.fori_loop(0, rows // 16, body, 0)


def place_items(t, fanout, lowest, members, me, routes_ref, in_ref, counts, normal_ref, stage):
    for k in range(fanout):
        group = routes_ref[t * fanout + k]
        slot = counts[group]
        counts[group] = slot + 1
        partner = (group ^ me) - lowest

        @pl.when(jnp.logical_and(partner >= 0, partner < members))
        def _():
            for q in range(KEEP):
                at = pl.multiple_of(in_ref[group * KEEP + q] * BLK, BLK)
                stage[partner, q, slot] = normal_ref[t, :, pl.ds(at, BLK)]


def send_stage(stage, outs, sems):
    copies = [
        pltpu.make_async_copy(stage.at[s], out, sems.at[s]) for s, out in enumerate(outs)
    ]
    for copy in copies:
        copy.start()
    for copy in copies:
        copy.wait()


def far_kernel(groups, fanout, windows, *refs):
    members = groups // 2
    me_ref, ends_ref, routes_ref, in_ref, gain_ref, own_ref, below_ref = refs[:7]
    normal_ref = refs[7]
    outs = refs[8 : 8 + members]
    ext, stage, counts, sems = refs[8 + members :]
    width = own_ref.shape[1]
    gain = gain_ref[...]

    def body(i, carry):
        at = pl.ds(pl.multiple_of(i * 16, 16), 16)
        ext[at, :] = normalize_rows(below_ref[at, :], gain, width)
        return carry

    lowest = ends_ref[0] + 1
    for w in range(1, windows):
        lowest = jnp.minimum(lowest, ends_ref[w] + 1)
    lax.fori_loop(jnp.minimum(lowest, LEN) // 16, LEN // 16, body, 0)
    ext[LEN:, :] = own_ref[:SEG, :]
    clear_counts(counts, groups)
    me = me_ref[0]
    segs_per_window = LEN // SEG
    last = own_ref.shape[0] - SEG
    sublane = lax.broadcasted_iota(jnp.int32, (SEG, width), 0)
    for w in range(windows):
        first = ends_ref[w] + 1
        offset = lax.rem(first, SEG)
        base = first - offset
        turn = lax.rem(SEG - offset, SEG)

        def take(j, low_rows, high_rows):
            t = w * segs_per_window + j
            rows = jnp.where(
                sublane < SEG - offset,
                pltpu.roll(low_rows, turn, 0),
                pltpu.roll(high_rows, turn, 0),
            )
            normal_ref[t] = rows.astype(jnp.bfloat16)
            place_items(
                t, fanout, groups - members, members, me, routes_ref, in_ref, counts,
                normal_ref, stage,
            )

        def from_below(j, carry):
            low = pl.multiple_of(base + j * SEG, SEG)
            take(j, ext[pl.ds(low, SEG), :], ext[pl.ds(low + SEG, SEG), :])
            return carry

        def from_own(j, carry):
            low = pl.multiple_of(base + j * SEG - LEN, SEG)
            high = pl.multiple_of(jnp.minimum(low + SEG, last), SEG)
            take(j, own_ref[pl.ds(low, SEG), :], own_ref[pl.ds(high, SEG), :])
            return carry

        split = jnp.clip((LEN - base) // SEG, 0, segs_per_window)
        lax.fori_loop(0, split, from_below, 0)
        lax.fori_loop(split, segs_per_window, from_own, 0)
    send_stage(stage, outs, sems)


def near_kernel(groups, fanout, *refs):
    members = groups // 2
    me_ref, routes_ref, in_ref, normal_ref = refs[:4]
    outs = refs[4 : 4 + members]
    stage, counts, sems = refs[4 + members :]
    clear_counts(counts, groups)
    me = me_ref[0]

    def body(t, carry):
        place_items(
            t, fanout, 0, members, me, routes_ref, in_ref, counts, normal_ref, stage
        )
        return carry

    lax.fori_loop(0, normal_ref.shape[0], body, 0)
    send_stage(stage, outs, sems)


def features_kernel(count, cap, *refs):
    xs = refs[:count]
    enc_ref, dec_ref, bias_ref, cut_ref, read_ref = refs[count : count + 5]
    outs = refs[count + 6 : 2 * count + 6]
    x_all, dec_acc, pull_acc, score_acc = refs[2 * count + 6 :]
    step = pl.program_id(0)
    rows = cap * SEG

    @pl.when(step == 0)
    def _():
        for i in range(count):
            for q in range(KEEP):
                x_all[i * rows : (i + 1) * rows, q * BLK : (q + 1) * BLK] = xs[i][q]
        dec_acc[...] = jnp.zeros_like(dec_acc)
        pull_acc[...] = jnp.zeros_like(pull_acc)
        score_acc[...] = jnp.zeros_like(score_acc)

    pre = (
        jnp.dot(x_all[...], enc_ref[...], preferred_element_type=jnp.float32) + bias_ref[...]
    )
    readout = read_ref[...]
    firing = jax.nn.sigmoid((pre - cut_ref[...]) * (1.0 / step_sharpness))
    active = pre * firing
    slope = (
        readout * (firing + active * (1.0 - firing) * (1.0 / step_sharpness))
    ).astype(jnp.bfloat16)
    dec_acc[...] += jnp.dot(
        active.astype(jnp.bfloat16), dec_ref[...], preferred_element_type=jnp.float32
    )
    pull_acc[...] += lax.dot_general(
        slope, enc_ref[...], (((1,), (1,)), ((), ())), preferred_element_type=jnp.float32
    )
    weighted = readout * active
    part = weighted[:, :BLK]
    for j in range(1, weighted.shape[1] // BLK):
        part = part + weighted[:, j * BLK : (j + 1) * BLK]
    score_acc[...] += part

    @pl.when(step == pl.num_programs(0) - 1)
    def _():
        lanes = lax.broadcasted_iota(jnp.int32, (SEG, BLK), 1)
        totals = jnp.sum(score_acc[...], axis=1, keepdims=True)
        for i in range(count):
            for q in range(KEEP):
                for acc, base in ((dec_acc, 0), (pull_acc, KEEP)):
                    tile = acc[i * rows : (i + 1) * rows, q * BLK : (q + 1) * BLK]
                    outs[i][(base + q) * cap : (base + q + 1) * cap] = tile.astype(
                        jnp.bfloat16
                    ).reshape(cap, SEG, BLK)
            marks = jnp.zeros((SEG, BLK), jnp.float32)
            for c in range(cap):
                at = i * rows + c * SEG
                marks = jnp.where(lanes == c, totals[at : at + SEG], marks)
            outs[i][2 * KEEP * cap] = marks.astype(jnp.bfloat16)


def combine_kernel(groups, cap, fanout, segments, final, *refs):
    members = groups // 4 if final else groups - groups // 4
    me_ref, routes_ref, in_ref, out_ref = refs[:4]
    backs = refs[4 : 4 + members]
    if final:
        recon_acc, grad_acc, marks_acc, normal_ref = refs[4 + members : 8 + members]
        recon_out, attr_out, score_ref = refs[8 + members : 11 + members]
        stage, recon_ref, attr_ref, out_sems, counts, sems = refs[14 + members :]
    else:
        bias_ref = refs[4 + members]
        recon_acc, grad_acc, score_ref = refs[5 + members : 8 + members]
        stage, counts, sems = refs[8 + members :]
    copies = [
        pltpu.make_async_copy(backs[s], stage.at[s], sems.at[s]) for s in range(members)
    ]
    for copy in copies:
        copy.start()
    clear_counts(counts, groups)
    me = me_ref[0]
    lowest = groups - members if final else 0
    for copy in copies:
        copy.wait()
    lane = lax.broadcasted_iota(jnp.int32, (SEG, BLK), 1)
    sublane = lax.broadcasted_iota(jnp.int32, (SEG, BLK), 0)
    per_row = BLK // SEG
    if not final:
        bias = jnp.broadcast_to(bias_ref[...], recon_acc.shape[1:])

    def one(t, carry):
        if not final:
            recon_acc[t] = bias
            grad_acc[t] = jnp.zeros_like(bias)
            score_ref[t] = jnp.zeros((SEG, BLK), jnp.float32)
        for k in range(fanout):
            group = routes_ref[t * fanout + k]
            slot = counts[group]
            counts[group] = slot + 1
            partner = (group ^ me) - lowest
            here = jnp.logical_and(partner >= 0, partner < members)

            @pl.when(here)
            def _():
                for q in range(KEEP):
                    at = pl.ds(pl.multiple_of(out_ref[group * KEEP + q] * BLK, BLK), BLK)
                    recon_acc[t, :, at] += stage[partner, q * cap + slot].astype(jnp.float32)
                    at = pl.ds(pl.multiple_of(in_ref[group * KEEP + q] * BLK, BLK), BLK)
                    grad_acc[t, :, at] += stage[partner, (KEEP + q) * cap + slot].astype(
                        jnp.float32
                    )
                marks = stage[partner, 2 * KEEP * cap].astype(jnp.float32)
                held = marks_acc if final else score_ref
                held[t] += jnp.where(lane == slot, marks, 0.0)

        if final:
            recon_ref[t] = recon_acc[t].astype(jnp.bfloat16)
            attr_ref[t] = (normal_ref[t].astype(jnp.float32) * grad_acc[t]).astype(
                jnp.bfloat16
            )
        return carry

    if not final:
        lax.fori_loop(0, segments, one, 0)
    else:
        step = segments // PIECES
        leaving = []
        for piece in range(PIECES):
            lax.fori_loop(piece * step, (piece + 1) * step, one, 0)
            at = pl.ds(piece * step, step)
            for i, (held, out) in enumerate(((recon_ref, recon_out), (attr_ref, attr_out))):
                leaving.append(
                    pltpu.make_async_copy(held.at[at], out.at[at], out_sems.at[i, piece])
                )
                leaving[-1].start()
        for row in range(segments // per_row):
            line = jnp.zeros((SEG, BLK), jnp.float32)
            for i in range(per_row):
                total = jnp.sum(marks_acc[row * per_row + i], axis=1, keepdims=True)
                line = jnp.where(lane == i * SEG + sublane, total, line)
            score_ref[row : row + 1, :] = jnp.sum(line, axis=0, keepdims=True)
        for copy in leaving:
            copy.wait()


def program(
    corpus,
    window_ends,
    norm_gain,
    routes,
    in_blocks,
    out_blocks,
    enc_weight,
    enc_bias,
    latent_cutoffs,
    dec_weight,
    readout,
    dec_bias,
):
    groups = lax.axis_size("seq")
    width = corpus.shape[1]
    windows = window_ends.shape[0]
    segments, fanout = routes.shape
    features = enc_weight.shape[1]
    cap = max(2, 2 * segments * fanout // groups)
    me = lax.axis_index("seq").astype(jnp.int32).reshape(1)
    below = lax.ppermute(corpus[-LEN:], "seq", [(i, i + 1) for i in range(groups - 1)])
    flat_routes = routes.reshape(-1)
    flat_in = in_blocks.reshape(-1)
    flat_out = out_blocks.reshape(-1)

    own = pl.pallas_call(
        own_kernel,
        out_shape=jax.ShapeDtypeStruct(corpus.shape, jnp.float32),
        in_specs=[VMEM] * 2,
        out_specs=VMEM,
        cost_estimate=pl.CostEstimate(
            flops=6 * corpus.size, bytes_accessed=6 * corpus.size, transcendentals=0
        ),
        compiler_params=pltpu.CompilerParams(vmem_limit_bytes=12 << 20),
        name="own",
    )(norm_gain.reshape(1, -1), corpus)
    half = groups // 2
    slots = jax.ShapeDtypeStruct((KEEP, cap, SEG, BLK), jnp.bfloat16)
    pack_scratch = [
        pltpu.VMEM((half, KEEP, cap, SEG, BLK), jnp.bfloat16),
        pltpu.SMEM((groups,), jnp.int32),
        pltpu.SemaphoreType.DMA((half,)),
    ]
    far = pl.pallas_call(
        functools.partial(far_kernel, groups, fanout, windows),
        out_shape=(jax.ShapeDtypeStruct((segments, SEG, width), jnp.bfloat16),)
        + (slots,) * half,
        in_specs=[SMEM] * 4 + [VMEM] * 3,
        out_specs=(VMEM,) + (ANY,) * half,
        scratch_shapes=[pltpu.VMEM((LEN + SEG, width), jnp.float32)] + pack_scratch,
        cost_estimate=pl.CostEstimate(flops=10_000_000, bytes_accessed=8_000_000, transcendentals=0),
        compiler_params=pltpu.CompilerParams(vmem_limit_bytes=16 << 20),
        name="far",
    )(me, window_ends, flat_routes, flat_in, norm_gain.reshape(1, -1), own, below)
    normal = far[0]
    near = pl.pallas_call(
        functools.partial(near_kernel, groups, fanout),
        out_shape=(slots,) * half,
        in_specs=[SMEM] * 3 + [VMEM],
        out_specs=(ANY,) * half,
        scratch_shapes=pack_scratch,
        cost_estimate=pl.CostEstimate(
            flops=10_000_000, bytes_accessed=4_000_000, transcendentals=0
        ),
        compiler_params=pltpu.CompilerParams(vmem_limit_bytes=8 << 20),
        name="near",
    )(me, flat_routes, flat_in, normal)
    outgoing = tuple(near) + tuple(far[1:])

    def exchange(block, pattern):
        if pattern == 0:
            return block
        return lax.ppermute(block, "seq", [(i, i ^ pattern) for i in range(groups)])

    quarter = groups // 4
    arrived = {}
    for s in send_order(groups):
        arrived[s] = exchange(outgoing[s], s)

    rows = cap * SEG
    tile = 512
    features_call = pl.pallas_call(
        functools.partial(features_kernel, quarter, cap),
        grid=(features // tile,),
        out_shape=(
            jax.ShapeDtypeStruct((2 * KEEP * cap + 1, SEG, BLK), jnp.bfloat16),
        )
        * quarter,
        in_specs=[pl.BlockSpec((KEEP, rows, BLK), lambda f: (0, 0, 0))] * quarter
        + [
            pl.BlockSpec((KEEP * BLK, tile), lambda f: (0, f)),
            pl.BlockSpec((tile, KEEP * BLK), lambda f: (f, 0)),
            pl.BlockSpec((1, tile), lambda f: (0, f)),
            pl.BlockSpec((1, tile), lambda f: (0, f)),
            pl.BlockSpec((1, tile), lambda f: (0, f)),
            ANY,
        ],
        out_specs=(
            pl.BlockSpec((2 * KEEP * cap + 1, SEG, BLK), lambda f: (0, 0, 0)),
        )
        * quarter,
        scratch_shapes=[
            pltpu.VMEM((quarter * rows, KEEP * BLK), jnp.bfloat16),
            pltpu.VMEM((quarter * rows, KEEP * BLK), jnp.float32),
            pltpu.VMEM((quarter * rows, KEEP * BLK), jnp.float32),
            pltpu.VMEM((quarter * rows, BLK), jnp.float32),
        ],
        cost_estimate=pl.CostEstimate(
            flops=6 * quarter * rows * KEEP * BLK * features,
            bytes_accessed=4 * KEEP * BLK * features,
            transcendentals=quarter * rows * features,
        ),
        compiler_params=pltpu.CompilerParams(vmem_limit_bytes=20 << 20),
        name="features",
    )
    returned = {}
    turn = me
    for part in [1, 2, 0, 3]:
        members = list(range(part * quarter, (part + 1) * quarter))
        results = features_call(
            *[arrived[s].reshape(KEEP, rows, BLK) for s in members],
            enc_weight,
            dec_weight,
            enc_bias.reshape(1, -1),
            latent_cutoffs.reshape(1, -1),
            readout.reshape(1, -1),
            turn,
        )
        turn = results[0]
        for s, result in zip(members, results):
            returned[s] = exchange(result, s)

    def combine(final, members, out_shape, in_specs, out_specs, scratch, aliases, *rest):
        return pl.pallas_call(
            functools.partial(combine_kernel, groups, cap, fanout, segments, final),
            out_shape=out_shape,
            in_specs=[SMEM] * 4 + [ANY] * len(members) + in_specs,
            out_specs=out_specs,
            input_output_aliases=aliases,
            scratch_shapes=[
                pltpu.VMEM((len(members), 2 * KEEP * cap + 1, SEG, BLK), jnp.bfloat16),
                *scratch,
                pltpu.SMEM((groups,), jnp.int32),
                pltpu.SemaphoreType.DMA((len(members),)),
            ],
            cost_estimate=pl.CostEstimate(
                flops=10_000_000, bytes_accessed=10_000_000, transcendentals=0
            ),
            compiler_params=pltpu.CompilerParams(vmem_limit_bytes=20 << 20),
            name="combine",
        )(
            me,
            flat_routes,
            flat_in,
            flat_out,
            *[returned[s] for s in members],
            *rest,
        )

    wide = jax.ShapeDtypeStruct((segments, SEG, width), jnp.float32)
    thin = jax.ShapeDtypeStruct((segments, SEG, width), jnp.bfloat16)
    marks = jax.ShapeDtypeStruct((segments, SEG, BLK), jnp.float32)
    parts = combine(
        False,
        range(groups - quarter),
        (wide, wide, marks),
        [VMEM],
        (VMEM,) * 3,
        [],
        {},
        dec_bias.reshape(1, -1),
    )
    first = 4 + quarter
    recon, attr, score = combine(
        True,
        range(groups - quarter, groups),
        (thin, thin, jax.ShapeDtypeStruct((segments * SEG // BLK, BLK), jnp.float32))
        + (wide, wide, marks),
        [VMEM] * 4,
        (ANY, ANY, VMEM) + (ANY,) * 3,
        [pltpu.VMEM((segments, SEG, width), jnp.bfloat16)] * 2
        + [pltpu.SemaphoreType.DMA((2, PIECES))],
        {first: 3, first + 1: 4, first + 2: 5},
        *parts,
        normal,
    )[:3]
    feature_score = score.reshape(-1)
    return (recon.reshape(-1, width), attr.reshape(-1, width), feature_score)


def solution(mesh):
    in_specs = (
        P(("grp", "seq"), None),
        P(("grp", "seq")),
        P(),
        P(("grp", "seq"), None),
        P(),
        P(),
        P(None, "seq"),
        P("seq"),
        P("seq"),
        P("seq", None),
        P("seq"),
        P(),
    )
    out_specs = (P(("grp", "seq"), None), P(("grp", "seq"), None), P(("grp", "seq")))
    return jax.shard_map(
        program, mesh=mesh, in_specs=in_specs, out_specs=out_specs, check_vma=False
    )
```

```python
import functools

import jax
import jax.numpy as jnp
from jax import lax
from jax.experimental import pallas as pl
from jax.experimental.pallas import tpu as pltpu
from jax.sharding import PartitionSpec as P


BLK = 128
KEEP = 7
LEN = 128
SEG = 8
step_sharpness = 0.1
norm_eps = 1e-06
PIECES = 4


SMEM = pl.BlockSpec(memory_space=pltpu.SMEM)
VMEM = pl.BlockSpec(memory_space=pltpu.VMEM)
ANY = pl.BlockSpec(memory_space=pl.ANY)


def quarters(groups):
    quarter = groups // 4
    return [list(range(part * quarter, (part + 1) * quarter)) for part in range(4)]


def send_order(groups):
    own, near, far, last = quarters(groups)
    return far[:1] + near + far[1:] + last + own[1:]


def clear_counts(counts, groups):
    def zero(i, carry):
        counts[i] = 0
        return carry

    lax.fori_loop(0, groups, zero, 0)


def normalize_rows(x, gain, width):
    x = x.astype(jnp.float32)
    mean = jnp.sum(x * x, axis=1, keepdims=True) * (1.0 / width)
    return (x * lax.rsqrt(mean + norm_eps) * gain).astype(jnp.bfloat16).astype(jnp.float32)


def own_kernel(gain_ref, corpus_ref, own_ref):
    rows, width = corpus_ref.shape
    gain = gain_ref[...]

    def body(i, carry):
        at = pl.ds(pl.multiple_of(i * 16, 16), 16)
        own_ref[at, :] = normalize_rows(corpus_ref[at, :], gain, width)
        return carry

    lax.fori_loop(0, rows // 16, body, 0)


def place_items(t, fanout, me, routes_ref, in_ref, counts, normal_ref, stage):
    for k in range(fanout):
        group = routes_ref[t * fanout + k]
        slot = counts[group]
        counts[group] = slot + 1
        partner = group ^ me
        for q in range(KEEP):
            at = pl.multiple_of(in_ref[group * KEEP + q] * BLK, BLK)
            stage[partner, q, slot] = normal_ref[t, :, pl.ds(at, BLK)]


def send_stage(stage, outs, sems):
    copies = [
        pltpu.make_async_copy(stage.at[s], out, sems.at[s]) for s, out in enumerate(outs)
    ]
    for copy in copies:
        copy.start()
    for copy in copies:
        copy.wait()


def pack_kernel(groups, fanout, windows, *refs):
    me_ref, ends_ref, routes_ref, in_ref, gain_ref, own_ref, below_ref = refs[:7]
    normal_ref = refs[7]
    outs = refs[8 : 8 + groups]
    ext, stage, counts, sems = refs[8 + groups :]
    width = own_ref.shape[1]
    gain = gain_ref[...]

    def body(i, carry):
        at = pl.ds(pl.multiple_of(i * 16, 16), 16)
        ext[at, :] = normalize_rows(below_ref[at, :], gain, width)
        return carry

    lowest = ends_ref[0] + 1
    for w in range(1, windows):
        lowest = jnp.minimum(lowest, ends_ref[w] + 1)
    lax.fori_loop(jnp.minimum(lowest, LEN) // 16, LEN // 16, body, 0)
    ext[LEN:, :] = own_ref[:SEG, :]
    clear_counts(counts, groups)
    me = me_ref[0]
    segs_per_window = LEN // SEG
    last = own_ref.shape[0] - SEG
    sublane = lax.broadcasted_iota(jnp.int32, (SEG, width), 0)
    for w in range(windows):
        first = ends_ref[w] + 1
        offset = lax.rem(first, SEG)
        base = first - offset
        turn = lax.rem(SEG - offset, SEG)

        def take(j, low_rows, high_rows):
            t = w * segs_per_window + j
            rows = jnp.where(
                sublane < SEG - offset,
                pltpu.roll(low_rows, turn, 0),
                pltpu.roll(high_rows, turn, 0),
            )
            normal_ref[t] = rows.astype(jnp.bfloat16)
            place_items(t, fanout, me, routes_ref, in_ref, counts, normal_ref, stage)

        def from_below(j, carry):
            low = pl.multiple_of(base + j * SEG, SEG)
            take(j, ext[pl.ds(low, SEG), :], ext[pl.ds(low + SEG, SEG), :])
            return carry

        def from_own(j, carry):
            low = pl.multiple_of(base + j * SEG - LEN, SEG)
            high = pl.multiple_of(jnp.minimum(low + SEG, last), SEG)
            take(j, own_ref[pl.ds(low, SEG), :], own_ref[pl.ds(high, SEG), :])
            return carry

        split = jnp.clip((LEN - base) // SEG, 0, segs_per_window)
        lax.fori_loop(0, split, from_below, 0)
        lax.fori_loop(split, segs_per_window, from_own, 0)
    send_stage(stage, outs, sems)


def features_kernel(count, cap, *refs):
    xs = refs[:count]
    enc_ref, dec_ref, bias_ref, cut_ref, read_ref = refs[count : count + 5]
    outs = refs[count + 6 : 2 * count + 6]
    x_all, dec_acc, pull_acc, score_acc = refs[2 * count + 6 :]
    step = pl.program_id(0)
    rows = cap * SEG

    @pl.when(step == 0)
    def _():
        for i in range(count):
            for q in range(KEEP):
                x_all[i * rows : (i + 1) * rows, q * BLK : (q + 1) * BLK] = xs[i][q]
        dec_acc[...] = jnp.zeros_like(dec_acc)
        pull_acc[...] = jnp.zeros_like(pull_acc)
        score_acc[...] = jnp.zeros_like(score_acc)

    pre = (
        jnp.dot(x_all[...], enc_ref[...], preferred_element_type=jnp.float32) + bias_ref[...]
    )
    readout = read_ref[...]
    firing = jax.nn.sigmoid((pre - cut_ref[...]) * (1.0 / step_sharpness))
    active = pre * firing
    slope = (
        readout * (firing + active * (1.0 - firing) * (1.0 / step_sharpness))
    ).astype(jnp.bfloat16)
    dec_acc[...] += jnp.dot(
        active.astype(jnp.bfloat16), dec_ref[...], preferred_element_type=jnp.float32
    )
    pull_acc[...] += lax.dot_general(
        slope, enc_ref[...], (((1,), (1,)), ((), ())), preferred_element_type=jnp.float32
    )
    weighted = readout * active
    part = weighted[:, :BLK]
    for j in range(1, weighted.shape[1] // BLK):
        part = part + weighted[:, j * BLK : (j + 1) * BLK]
    score_acc[...] += part

    @pl.when(step == pl.num_programs(0) - 1)
    def _():
        lanes = lax.broadcasted_iota(jnp.int32, (SEG, BLK), 1)
        totals = jnp.sum(score_acc[...], axis=1, keepdims=True)
        for i in range(count):
            for q in range(KEEP):
                for acc, base in ((dec_acc, 0), (pull_acc, KEEP)):
                    tile = acc[i * rows : (i + 1) * rows, q * BLK : (q + 1) * BLK]
                    outs[i][(base + q) * cap : (base + q + 1) * cap] = tile.astype(
                        jnp.bfloat16
                    ).reshape(cap, SEG, BLK)
            marks = jnp.zeros((SEG, BLK), jnp.float32)
            for c in range(cap):
                at = i * rows + c * SEG
                marks = jnp.where(lanes == c, totals[at : at + SEG], marks)
            outs[i][2 * KEEP * cap] = marks.astype(jnp.bfloat16)


def combine_kernel(groups, cap, fanout, segments, final, *refs):
    members = groups // 4 if final else groups - groups // 4
    me_ref, routes_ref, in_ref, out_ref = refs[:4]
    backs = refs[4 : 4 + members]
    if final:
        recon_acc, grad_acc, marks_acc, normal_ref = refs[4 + members : 8 + members]
        recon_out, attr_out, score_ref = refs[8 + members : 11 + members]
        stage, recon_ref, attr_ref, out_sems, counts, sems = refs[14 + members :]
    else:
        bias_ref = refs[4 + members]
        recon_acc, grad_acc, score_ref = refs[5 + members : 8 + members]
        stage, counts, sems = refs[8 + members :]
    copies = [
        pltpu.make_async_copy(backs[s], stage.at[s], sems.at[s]) for s in range(members)
    ]
    for copy in copies:
        copy.start()
    clear_counts(counts, groups)
    me = me_ref[0]
    lowest = groups - members if final else 0
    for copy in copies:
        copy.wait()
    lane = lax.broadcasted_iota(jnp.int32, (SEG, BLK), 1)
    sublane = lax.broadcasted_iota(jnp.int32, (SEG, BLK), 0)
    per_row = BLK // SEG
    if not final:
        bias = jnp.broadcast_to(bias_ref[...], recon_acc.shape[1:])

    def one(t, carry):
        if not final:
            recon_acc[t] = bias
            grad_acc[t] = jnp.zeros_like(bias)
            score_ref[t] = jnp.zeros((SEG, BLK), jnp.float32)
        for k in range(fanout):
            group = routes_ref[t * fanout + k]
            slot = counts[group]
            counts[group] = slot + 1
            partner = (group ^ me) - lowest
            here = jnp.logical_and(partner >= 0, partner < members)

            @pl.when(here)
            def _():
                for q in range(KEEP):
                    at = pl.ds(pl.multiple_of(out_ref[group * KEEP + q] * BLK, BLK), BLK)
                    recon_acc[t, :, at] += stage[partner, q * cap + slot].astype(jnp.float32)
                    at = pl.ds(pl.multiple_of(in_ref[group * KEEP + q] * BLK, BLK), BLK)
                    grad_acc[t, :, at] += stage[partner, (KEEP + q) * cap + slot].astype(
                        jnp.float32
                    )
                marks = stage[partner, 2 * KEEP * cap].astype(jnp.float32)
                held = marks_acc if final else score_ref
                held[t] += jnp.where(lane == slot, marks, 0.0)

        if final:
            recon_ref[t] = recon_acc[t].astype(jnp.bfloat16)
            attr_ref[t] = (normal_ref[t].astype(jnp.float32) * grad_acc[t]).astype(
                jnp.bfloat16
            )
        return carry

    if not final:
        lax.fori_loop(0, segments, one, 0)
    else:
        step = segments // PIECES
        leaving = []
        for piece in range(PIECES):
            lax.fori_loop(piece * step, (piece + 1) * step, one, 0)
            at = pl.ds(piece * step, step)
            for i, (held, out) in enumerate(((recon_ref, recon_out), (attr_ref, attr_out))):
                leaving.append(
                    pltpu.make_async_copy(held.at[at], out.at[at], out_sems.at[i, piece])
                )
                leaving[-1].start()
        for row in range(segments // per_row):
            line = jnp.zeros((SEG, BLK), jnp.float32)
            for i in range(per_row):
                total = jnp.sum(marks_acc[row * per_row + i], axis=1, keepdims=True)
                line = jnp.where(lane == i * SEG + sublane, total, line)
            score_ref[row : row + 1, :] = jnp.sum(line, axis=0, keepdims=True)
        for copy in leaving:
            copy.wait()


def program(
    corpus,
    window_ends,
    norm_gain,
    routes,
    in_blocks,
    out_blocks,
    enc_weight,
    enc_bias,
    latent_cutoffs,
    dec_weight,
    readout,
    dec_bias,
):
    groups = lax.axis_size("seq")
    width = corpus.shape[1]
    windows = window_ends.shape[0]
    segments, fanout = routes.shape
    features = enc_weight.shape[1]
    cap = max(2, 2 * segments * fanout // groups)
    me = lax.axis_index("seq").astype(jnp.int32).reshape(1)
    below = lax.ppermute(corpus[-LEN:], "seq", [(i, i + 1) for i in range(groups - 1)])
    flat_routes = routes.reshape(-1)
    flat_in = in_blocks.reshape(-1)
    flat_out = out_blocks.reshape(-1)

    own = pl.pallas_call(
        own_kernel,
        out_shape=jax.ShapeDtypeStruct(corpus.shape, jnp.float32),
        in_specs=[VMEM] * 2,
        out_specs=VMEM,
        cost_estimate=pl.CostEstimate(
            flops=6 * corpus.size, bytes_accessed=6 * corpus.size, transcendentals=0
        ),
        compiler_params=pltpu.CompilerParams(vmem_limit_bytes=12 << 20),
        name="own",
    )(norm_gain.reshape(1, -1), corpus)
    packed = pl.pallas_call(
        functools.partial(pack_kernel, groups, fanout, windows),
        out_shape=(jax.ShapeDtypeStruct((segments, SEG, width), jnp.bfloat16),)
        + (jax.ShapeDtypeStruct((KEEP, cap, SEG, BLK), jnp.bfloat16),) * groups,
        in_specs=[SMEM] * 4 + [VMEM] * 3,
        out_specs=(VMEM,) + (ANY,) * groups,
        scratch_shapes=[
            pltpu.VMEM((LEN + SEG, width), jnp.float32),
            pltpu.VMEM((groups, KEEP, cap, SEG, BLK), jnp.bfloat16),
            pltpu.SMEM((groups,), jnp.int32),
            pltpu.SemaphoreType.DMA((groups,)),
        ],
        cost_estimate=pl.CostEstimate(flops=10_000_000, bytes_accessed=8_000_000, transcendentals=0),
        compiler_params=pltpu.CompilerParams(vmem_limit_bytes=16 << 20),
        name="pack",
    )(me, window_ends, flat_routes, flat_in, norm_gain.reshape(1, -1), own, below)
    normal, outgoing = packed[0], packed[1:]

    def exchange(block, pattern):
        if pattern == 0:
            return block
        return lax.ppermute(block, "seq", [(i, i ^ pattern) for i in range(groups)])

    quarter = groups // 4
    arrived = {0: outgoing[0]}
    for s in send_order(groups):
        arrived[s] = exchange(outgoing[s], s)

    rows = cap * SEG
    tile = 512
    features_call = pl.pallas_call(
        functools.partial(features_kernel, quarter, cap),
        grid=(features // tile,),
        out_shape=(
            jax.ShapeDtypeStruct((2 * KEEP * cap + 1, SEG, BLK), jnp.bfloat16),
        )
        * quarter,
        in_specs=[pl.BlockSpec((KEEP, rows, BLK), lambda f: (0, 0, 0))] * quarter
        + [
            pl.BlockSpec((KEEP * BLK, tile), lambda f: (0, f)),
            pl.BlockSpec((tile, KEEP * BLK), lambda f: (f, 0)),
            pl.BlockSpec((1, tile), lambda f: (0, f)),
            pl.BlockSpec((1, tile), lambda f: (0, f)),
            pl.BlockSpec((1, tile), lambda f: (0, f)),
            ANY,
        ],
        out_specs=(
            pl.BlockSpec((2 * KEEP * cap + 1, SEG, BLK), lambda f: (0, 0, 0)),
        )
        * quarter,
        scratch_shapes=[
            pltpu.VMEM((quarter * rows, KEEP * BLK), jnp.bfloat16),
            pltpu.VMEM((quarter * rows, KEEP * BLK), jnp.float32),
            pltpu.VMEM((quarter * rows, KEEP * BLK), jnp.float32),
            pltpu.VMEM((quarter * rows, BLK), jnp.float32),
        ],
        cost_estimate=pl.CostEstimate(
            flops=6 * quarter * rows * KEEP * BLK * features,
            bytes_accessed=4 * KEEP * BLK * features,
            transcendentals=quarter * rows * features,
        ),
        compiler_params=pltpu.CompilerParams(vmem_limit_bytes=20 << 20),
        name="features",
    )
    returned = {}
    turn = me
    for part in [1, 2, 0, 3]:
        members = list(range(part * quarter, (part + 1) * quarter))
        results = features_call(
            *[arrived[s].reshape(KEEP, rows, BLK) for s in members],
            enc_weight,
            dec_weight,
            enc_bias.reshape(1, -1),
            latent_cutoffs.reshape(1, -1),
            readout.reshape(1, -1),
            turn,
        )
        turn = results[0]
        for s, result in zip(members, results):
            returned[s] = exchange(result, s)

    def combine(final, members, out_shape, in_specs, out_specs, scratch, aliases, *rest):
        return pl.pallas_call(
            functools.partial(combine_kernel, groups, cap, fanout, segments, final),
            out_shape=out_shape,
            in_specs=[SMEM] * 4 + [ANY] * len(members) + in_specs,
            out_specs=out_specs,
            input_output_aliases=aliases,
            scratch_shapes=[
                pltpu.VMEM((len(members), 2 * KEEP * cap + 1, SEG, BLK), jnp.bfloat16),
                *scratch,
                pltpu.SMEM((groups,), jnp.int32),
                pltpu.SemaphoreType.DMA((len(members),)),
            ],
            cost_estimate=pl.CostEstimate(
                flops=10_000_000, bytes_accessed=10_000_000, transcendentals=0
            ),
            compiler_params=pltpu.CompilerParams(vmem_limit_bytes=20 << 20),
            name="combine",
        )(
            me,
            flat_routes,
            flat_in,
            flat_out,
            *[returned[s] for s in members],
            *rest,
        )

    wide = jax.ShapeDtypeStruct((segments, SEG, width), jnp.float32)
    thin = jax.ShapeDtypeStruct((segments, SEG, width), jnp.bfloat16)
    marks = jax.ShapeDtypeStruct((segments, SEG, BLK), jnp.float32)
    parts = combine(
        False,
        range(groups - quarter),
        (wide, wide, marks),
        [VMEM],
        (VMEM,) * 3,
        [],
        {},
        dec_bias.reshape(1, -1),
    )
    first = 4 + quarter
    recon, attr, score = combine(
        True,
        range(groups - quarter, groups),
        (thin, thin, jax.ShapeDtypeStruct((segments * SEG // BLK, BLK), jnp.float32))
        + (wide, wide, marks),
        [VMEM] * 4,
        (ANY, ANY, VMEM) + (ANY,) * 3,
        [pltpu.VMEM((segments, SEG, width), jnp.bfloat16)] * 2
        + [pltpu.SemaphoreType.DMA((2, PIECES))],
        {first: 3, first + 1: 4, first + 2: 5},
        *parts,
        normal,
    )[:3]
    feature_score = score.reshape(-1)
    return (recon.reshape(-1, width), attr.reshape(-1, width), feature_score)


def solution(mesh):
    in_specs = (
        P(("grp", "seq"), None),
        P(("grp", "seq")),
        P(),
        P(("grp", "seq"), None),
        P(),
        P(),
        P(None, "seq"),
        P("seq"),
        P("seq"),
        P("seq", None),
        P("seq"),
        P(),
    )
    out_specs = (P(("grp", "seq"), None), P(("grp", "seq"), None), P(("grp", "seq")))
    return jax.shard_map(
        program, mesh=mesh, in_specs=in_specs, out_specs=out_specs, check_vma=False
    )
```
